32 devices in a mesh: gx: 4 (over y, x), gy: 8 (over z, core).
Axes of the slice: x: 2, y: 2, z: 4, core: 2. Of those that a mesh axis runs over, the one named last changes fastest.
Arguments:
- element_fields: bfloat16 [16384, 5, 512], P(('gx', 'gy')), may hold values from -6 to 6
- ref_coords: float32 [3, 65536], P(None, ('gx', 'gy')), may hold values from -1 to 1
- local_element: int32 [65536], P(('gx', 'gy')), may hold values from 0 to 511
- owner: int32 [65536, 1], P(('gx', 'gy')), may hold values from 0 to 31; in each aligned block of 2048 rows (0 to 2047, 2048 to 4095, ...) at most 256 rows name the same one
- point_angle: float32 [65536], P(('gx', 'gy')), may hold values from -3.140625 to 3.140625
- point_axial: float32 [65536], P(('gx', 'gy')), may hold values from 0 to 8
- panel_weight: float32 [65536], P(('gx', 'gy')), may hold values from 0.5 to 2
- obs_radius: float32 [256], replicated, may hold values from 3 to 30
- obs_angle: float32 [256], replicated, may hold values from -3.140625 to 3.140625
- obs_axial: float32 [256], replicated, may hold values from -8 to 16
- step_phase: float32 [32], replicated, may hold values from -3.140625 to 3.140625
- observer_slot: int32 [256], replicated, may hold values from 0 to 255, each once
- prior_spectra: float32 [2, 32, 256], P(None, None, ('gx', 'gy')), may hold values from -6 to 6
Outputs:
- surface_values: float32 [5, 65536], P(None, ('gx', 'gy'))
- spectra: float32 [2, 32, 256], P(None, None, ('gx', 'gy'))
The draws below stay inside these ranges and needn't reach their ends.
Inputs may be any that keep to these rules, and one draw needn't show every extreme that they name: Among the points of one device at most 256 have the same owner, and in every draw some device has exactly 256 points owned by one device. `observer_slot`: each output column is named by exactly one observer.
All inputs are finite; a program needn't handle non-finite values.
Results may differ from the reference program's by a relative error of at most 0.0003.
Values sent between devices are 32-bit elements; how exact they have to be, the bound alone decides.
A program may use at most 64 MiB of HBM per device.

```python
import math
import jax
import jax.numpy as jnp
import numpy as np
from jax import lax

NODES = 512
FIELDS = 5
NOBS = 256
NFREQ = 32
ELEM_DEV = 512
PTS_DEV = 2048
ELEMENTS = 16384
POINTS = 65536
CAP = 256
DEVICES = 32


def plant(values, rng, low, high):
    extent = values.shape
    place = [jax.random.randint(jax.random.fold_in(rng, axis), (), 0, extent[axis]) for axis in range(len(extent))]
    values = values.at[tuple(place)].set(low)
    longest = extent.index(max(extent))
    place[longest] = (place[longest] + 1) % extent[longest]
    return values.at[tuple(place)].set(high)


def block_scale(key, shape, shards, low, top_value):
    factor_of, own = 1.0, jax.random.fold_in(key, 6)
    for axis_at, shards_of in shards:
        draws = jnp.exp(jax.random.uniform(jax.random.fold_in(own, axis_at), (shards_of,), jnp.float32, low / len(shards), top_value / len(shards)))
        factor_of = factor_of * jnp.repeat(draws, shape[axis_at] // shards_of).reshape([-1 if axis == axis_at else 1 for axis in range(len(shape))])
    return factor_of


def routed_block(key, own, number, rows, number_of, top, reach, slope):
    ranking = jax.random.permutation(key, number_of)
    heavy_load, usual = portions_of(number_of, rows * top, reach, slope, True), portions_of(number_of, rows * top, reach, slope, False)
    places = jnp.arange(number_of)

    def named(tallies, offset_by):
        used = int((tallies > 0).sum())
        fixed = max(1, used // 4)
        moved = fixed + (places - fixed + offset_by * (used - fixed)) % max(1, number_of - fixed)
        return jnp.zeros((number_of,), jnp.int32).at[ranking[jnp.where(places < fixed, places, moved)]].set(jnp.asarray(tallies, jnp.int32))

    tallies = jnp.where(number % 4 == 0, named(heavy_load, number // 4), named(usual, number - number // 4 - 1))
    mixed = jax.random.permutation(jax.random.fold_in(own, 3), number_of)
    giver, taker = mixed[0:number_of // 2 * 2:2], mixed[1:number_of // 2 * 2:2]
    margin = jnp.minimum(tallies[giver] - 1, reach - tallies[taker]) // 2
    margin = jnp.where((giver == ranking[0]) | (taker == ranking[0]) | (tallies[taker] == 0), 0, jnp.maximum(margin, 0))
    moved = jax.random.randint(jax.random.fold_in(own, 4), (number_of // 2,), 0, 1 << 20) % (margin + 1)
    tallies = tallies.at[giver].add(-moved).at[taker].add(moved)
    items = jnp.searchsorted(jnp.cumsum(tallies), jnp.arange(rows * top), side="right").astype(jnp.int32)
    listing = items.reshape(top, rows).T
    listing = listing[jax.random.permutation(jax.random.fold_in(own, 1), rows)]
    offset_by = jax.random.randint(jax.random.fold_in(own, 2), (rows, 1), 0, top)
    return jnp.take_along_axis(listing, (jnp.arange(top)[None, :] + offset_by) % top, axis=1)


def portions_of(amount, total, most, slope, full):
    loads = [(1 << 20) // math.isqrt(standing ** slope) + 1 for standing in range(1, amount + 1)]
    largest = most if full else min(most, max(-(-total // amount), total * loads[0] // sum(loads)))
    least = 1 if total - largest >= amount - 1 else 0
    holding, rest = [largest] + [least] * (amount - 1), total - largest - least * (amount - 1)
    while rest > 0:
        movable = [i for i in range(1, amount) if holding[i] < largest] or [i for i in range(1, amount) if holding[i] < most]
        mass, left = sum([loads[i] for i in movable]), rest
        for i in movable:
            extra = min(most - holding[i], max(1, left * loads[i] // mass), rest)
            holding[i] = holding[i] + extra
            rest = rest - extra
    return np.array(holding)


def normal_values(own_key, dims, width, bound, shards=(), kind=jnp.bfloat16):
    result = jax.random.normal(own_key, dims, jnp.float32) * width
    if len(shards) > 0:
        result = block_scale(own_key, dims, shards, -0.22, 0.18) * result
    return jnp.clip(result, min=-bound, max=bound).astype(kind)


def setup_inputs(seed: int = 0) -> dict:
    arg_keys = jax.random.split(jax.random.key(seed), 14)
    element_fields = normal_values(arg_keys[0], (ELEMENTS, FIELDS, NODES), 1.0, 6.0, ((0, 32),))
    ref_coords = jnp.clip(jax.random.uniform(arg_keys[1], (3, POINTS), jnp.float32, -1.0, 1.0) * block_scale(arg_keys[1], (3, POINTS), ((1, 32),), -0.4, 0.0), -1.0, 1.0)
    local_element = plant(jax.random.randint(arg_keys[2], (POINTS,), 0, ELEM_DEV), jax.random.fold_in(arg_keys[2], 1), 0, ELEM_DEV - 1).astype(jnp.int32)
    owner_keys = jax.random.split(jax.random.fold_in(arg_keys[3], 1), POINTS // PTS_DEV)
    owner_turns = jax.random.permutation(jax.random.fold_in(arg_keys[3], 3), POINTS // PTS_DEV)
    owner = jax.vmap(lambda own, number: routed_block(jax.random.fold_in(arg_keys[3], 2), own, number, PTS_DEV, DEVICES, 1, CAP, 2))(owner_keys, owner_turns).reshape((POINTS, 1))
    point_angle = jnp.clip(jax.random.uniform(arg_keys[4], (POINTS,), jnp.float32, -3.140625, 3.140625), -3.140625, 3.140625)
    point_axial = jnp.clip(8.0 * jax.random.uniform(arg_keys[5], (POINTS,), jnp.float32) ** block_scale(arg_keys[5], (POINTS,), ((0, 32),), -0.2, 0.2), 0.0, 8.0)
    panel_weight = jnp.clip(jnp.exp(math.log(2.0) - 1.3862944 * jax.random.uniform(arg_keys[6], (POINTS,), jnp.float32) ** block_scale(arg_keys[6], (POINTS,), ((0, 32),), -0.2, 0.2)), 0.5, 2.0)
    obs_radius = jnp.clip(jnp.exp(jax.random.uniform(arg_keys[7], (NOBS,), jnp.float32, math.log(3.0), math.log(30.0))), 3.0, 30.0)
    obs_angle = jnp.clip(jax.random.uniform(arg_keys[8], (NOBS,), jnp.float32, -3.140625, 3.140625), -3.140625, 3.140625)
    obs_axial = jnp.clip(jax.random.uniform(arg_keys[9], (NOBS,), jnp.float32, -8.0, 16.0), -8.0, 16.0)
    step_phase = jnp.clip(jax.random.uniform(arg_keys[10], (NFREQ,), jnp.float32, -3.140625, 3.140625), -3.140625, 3.140625)
    observer_slot = jax.random.permutation(arg_keys[11], NOBS).astype(jnp.int32)
    prior_spectra = normal_values(arg_keys[12], (2, NFREQ, NOBS), 1.0, 6.0, ((2, 32),), jnp.float32)
    return dict(element_fields=element_fields, ref_coords=ref_coords, local_element=local_element, owner=owner, point_angle=point_angle, point_axial=point_axial, panel_weight=panel_weight, obs_radius=obs_radius, obs_angle=obs_angle, obs_axial=obs_axial, step_phase=step_phase, observer_slot=observer_slot, prior_spectra=prior_spectra)


gll_nodes = np.array([-1.0, -0.8717401485096066, -0.5917001814331423, -0.2092992179024789, 0.2092992179024789, 0.5917001814331423, 0.8717401485096066, 1.0])
omega_base = 0.25

def lagrange(coord):
    columns = []
    for first in range(8):
        product = jnp.ones_like(coord)
        divisor = 1.0
        for second in range(8):
            if second != first:
                product = product * (coord - float(gll_nodes[second]))
                divisor = divisor * (gll_nodes[first] - gll_nodes[second])
        columns.append(product * float(1.0 / divisor))
    return jnp.stack(columns)

def node_weights(coords):
    along_r = lagrange(coords[0])
    along_s = lagrange(coords[1])
    along_t = lagrange(coords[2])
    pair_rs = along_r[:, None, :] * along_s[None, :, :]
    return (pair_rs[:, :, None, :] * along_t[None, None, :, :]).reshape(512, coords.shape[1])

def interpolate(fields, elem_ids, coords):
    weights = node_weights(coords)
    gathered = jnp.take(fields, elem_ids, axis=0).astype(jnp.float32)
    return jnp.einsum('nfq,qn->fn', gathered, weights)

def spectra_terms(values, angle, axial, weight, obs_radius, obs_angle, obs_axial, step_phase, norm_scale):
    cos_p = jnp.cos(angle)
    sin_p = jnp.sin(angle)
    step_x = (obs_radius * jnp.cos(obs_angle))[None, :] - cos_p[:, None]
    step_y = (obs_radius * jnp.sin(obs_angle))[None, :] - sin_p[:, None]
    step_z = obs_axial[None, :] - axial[:, None]
    distance = jnp.sqrt(step_x * step_x + step_y * step_y + step_z * step_z)
    density = values[0]
    vel_x = values[1]
    vel_y = values[2]
    vel_z = values[3]
    pressure = values[4]
    mass_flux = density * (vel_x * cos_p + vel_y * sin_p)
    radial = (step_x * cos_p[:, None] + step_y * sin_p[:, None]) / distance
    radial_vel = (vel_x[:, None] * step_x + vel_y[:, None] * step_y + vel_z[:, None] * step_z) / distance
    amplitude = weight[:, None] * (mass_flux[:, None] + pressure[:, None] * radial + mass_flux[:, None] * radial_vel) * obs_radius[None, :] / distance * norm_scale
    harmonic = omega_base * jnp.arange(1, step_phase.shape[0] + 1, dtype=jnp.float32)
    phases = distance[:, :, None] * harmonic[None, None, :] + step_phase[None, None, :]
    cos_sum = lax.optimization_barrier(jnp.sum(amplitude[:, :, None] * jnp.cos(phases), axis=0)).T
    sin_sum = -lax.optimization_barrier(jnp.sum(amplitude[:, :, None] * jnp.sin(phases), axis=0)).T
    return jnp.stack([cos_sum, sin_sum])

def reference(element_fields, ref_coords, local_element, owner, point_angle, point_axial, panel_weight, obs_radius, obs_angle, obs_axial, step_phase, observer_slot, prior_spectra):
    global_ids = (owner[:, 0] * ELEM_DEV + local_element).astype(jnp.int32)
    block_rows = math.gcd(POINTS, 2048)
    block_count = POINTS // block_rows

    def sample(pieces):
        return interpolate(element_fields, pieces[0], pieces[1])
    sampled = lax.map(sample, (global_ids.reshape(block_count, block_rows), ref_coords.reshape(3, block_count, block_rows).transpose(1, 0, 2)))
    surface_values = sampled.transpose(1, 0, 2).reshape(FIELDS, POINTS)
    norm_scale = 1.0 / math.sqrt(POINTS)

    def accumulate(running, pieces):
        return (running + spectra_terms(pieces[0], pieces[1], pieces[2], pieces[3], obs_radius, obs_angle, obs_axial, step_phase, norm_scale), None)
    starting = jnp.zeros((2, NFREQ, NOBS), jnp.float32)
    summed, unused = lax.scan(accumulate, starting, (surface_values.reshape(FIELDS, block_count, block_rows).transpose(1, 0, 2), point_angle.reshape(block_count, block_rows), point_axial.reshape(block_count, block_rows), panel_weight.reshape(block_count, block_rows)))
    placed = jnp.zeros_like(summed).at[:, :, observer_slot].set(summed)
    return (surface_values, prior_spectra + placed)
```

```python
import functools
import math

import jax
import jax.numpy as jnp
import numpy as np
from jax import lax
from jax.experimental import pallas as pl
from jax.experimental.pallas import tpu as pltpu
from jax.sharding import PartitionSpec as P

FIELDS = 5
AXES = ("gx", "gy")
F32 = jnp.float32
BF16 = jnp.bfloat16
BASIS = 8

gll_nodes = np.array(
    [
        -1.0,
        -0.8717401485096066,
        -0.5917001814331423,
        -0.2092992179024789,
        0.2092992179024789,
        0.5917001814331423,
        0.8717401485096066,
        1.0,
    ]
)
gll_scale = np.array(
    [1.0 / np.prod([gll_nodes[i] - gll_nodes[m] for m in range(8) if m != i]) for i in range(8)]
)
omega_base = 0.25


def three_parts(x):
    high = x.astype(BF16)
    rest = x - high.astype(F32)
    middle = rest.astype(BF16)
    low = (rest - middle.astype(F32)).astype(BF16)
    return high, middle, low


def contract_last(a, b):
    return lax.dot_general(a, b, (((1,), (1,)), ((), ())), preferred_element_type=F32)


def pack_kernel(devices, cap, target_ref, ids_ref, coords_ref, send_ref, rank_ref):
    points = target_ref.shape[1]
    width = math.gcd(points, 512)
    before = (
        lax.broadcasted_iota(jnp.int32, (width, width), 0)
        < lax.broadcasted_iota(jnp.int32, (width, width), 1)
    )
    before = jnp.where(before, 1.0, 0.0).astype(BF16)
    offset = jnp.zeros((devices, 1), F32)
    sums = [jnp.zeros((devices, cap), F32) for _ in range(4)]
    for block in range(points // width):
        lanes = slice(block * width, (block + 1) * width)
        mine = target_ref[:, lanes] == lax.broadcasted_iota(jnp.int32, (devices, width), 0)
        hot = jnp.where(mine, 1.0, 0.0)
        hot_half = hot.astype(BF16)
        within = jnp.dot(hot_half, before, preferred_element_type=F32) + offset
        rank = jnp.sum(hot * within, axis=0, keepdims=True).astype(jnp.int32)
        offset = offset + jnp.sum(hot, axis=1, keepdims=True)
        rank_ref[:, lanes] = rank
        spot = jnp.where(lax.broadcasted_iota(jnp.int32, (cap, width), 0) == rank, 1.0, 0.0)
        spot = spot.astype(BF16)
        for entry in range(4):
            if entry == 0:
                row = ids_ref[:, lanes].astype(F32)
            else:
                row = coords_ref[entry - 1 : entry, lanes]
            for part in three_parts(row * hot):
                sums[entry] = sums[entry] + contract_last(part, spot)
    for entry in range(4):
        send_ref[:, entry, :] = sums[entry]


def interp_kernel(ids_ref, recv_ref, expand_ref, fields_ref, out_ref, table, weights):
    devices, _, cap = recv_ref.shape
    block = min(cap, 128)
    elements = fields_ref.shape[0]

    def widen(e, carry):
        table[e, 0:FIELDS, :] = fields_ref[e].astype(F32)
        return carry

    lax.fori_loop(0, elements, widen, 0, unroll=8)
    node = lax.broadcasted_iota(jnp.int32, (8, block), 0)
    lane = lax.broadcasted_iota(jnp.int32, (FIELDS, block), 1)
    scale = jnp.zeros((8, block), F32)
    for i in range(8):
        scale = jnp.where(node == i, float(gll_scale[i]), scale)

    def source(s, carry):
        for half in range(cap // block):
            lanes = slice(half * block, (half + 1) * block)
            bases = []
            for axis in range(3):
                x = recv_ref[s, axis + 1 : axis + 2, lanes]
                product = scale
                for m in range(8):
                    product = product * jnp.where(node == m, 1.0, x - float(gll_nodes[m]))
                bases.append(product)
            stacked = jnp.concatenate(bases, axis=0)
            parts = jnp.concatenate([p.astype(F32) for p in three_parts(stacked)], axis=0)
            parts = parts.T.astype(BF16)
            wide = jnp.dot(parts, expand_ref[...], preferred_element_type=F32)
            pair = wide[:, 512:640] * wide[:, 640:768]
            for quarter in range(4):
                columns = slice(quarter * 128, (quarter + 1) * 128)
                weights[half, :, columns] = wide[:, columns] * pair
            result = jnp.zeros((FIELDS, block), F32)
            for p in range(block):
                e = ids_ref[s * cap + half * block + p]
                total = None
                for quarter in range(4):
                    columns = slice(quarter * 128, (quarter + 1) * 128)
                    term = table[e, 0:FIELDS, columns] * weights[half, p : p + 1, columns]
                    total = term if total is None else total + term
                value = jnp.sum(total, axis=1, keepdims=True)
                result = jnp.where(lane == p, value, result)
            out_ref[s, :, lanes] = result
        return carry

    lax.fori_loop(0, devices, source, 0)


def sincos(angle):
    turns = jnp.floor(angle * float(2.0 / math.pi) + 0.5)
    r = angle - turns * 1.5703125
    r = r - turns * 4.837512969970703125e-4
    r = r - turns * 7.54978995489188e-8
    z = r * r
    sine = ((-1.9515295891e-4 * z + 8.3321608736e-3) * z - 1.6666654611e-1) * z * r + r
    cosine = (
        (2.443315711809948e-5 * z - 1.388731625493765e-3) * z + 4.166664568298827e-2
    ) * z * z + (1.0 - 0.5 * z)
    quadrant = turns.astype(jnp.int32)
    odd = (quadrant & 1) == 1
    first = jnp.where(odd, sine, cosine)
    second = jnp.where(odd, cosine, sine)
    first = jnp.where(((quadrant + 1) & 2) == 2, -first, first)
    second = jnp.where((quadrant & 2) == 2, -second, second)
    return first, second


def spectra_kernel(
    norm_scale,
    replies_ref,
    target_ref,
    rank_ref,
    point_ref,
    obs_x_ref,
    obs_y_ref,
    obs_z_ref,
    surface_ref,
    sums_ref,
    rows,
    acc,
):
    devices, _, cap = replies_ref.shape
    points = target_ref.shape[1]
    width = math.gcd(points, 512)
    parts = [three_parts(replies_ref[:, f, :]) for f in range(FIELDS)]
    stacked = jnp.concatenate([p for triple in parts for p in triple], axis=0)
    for block in range(points // width):
        lanes = slice(block * width, (block + 1) * width)
        mine = target_ref[:, lanes] == lax.broadcasted_iota(jnp.int32, (devices, width), 0)
        spot = jnp.where(
            lax.broadcasted_iota(jnp.int32, (cap, width), 0) == rank_ref[:, lanes], 1.0, 0.0
        ).astype(BF16)
        found = jnp.dot(stacked, spot, preferred_element_type=F32)
        found = found.reshape(FIELDS, 3, devices, width)
        values = []
        for f in range(FIELDS):
            whole = (found[f, 0] + found[f, 1]) + found[f, 2]
            value = jnp.sum(jnp.where(mine, whole, 0.0), axis=0, keepdims=True)
            surface_ref[f : f + 1, lanes] = value
            values.append(value)
        density, vel_x, vel_y, vel_z, pressure = values
        cos_p = point_ref[0:1, lanes]
        sin_p = point_ref[1:2, lanes]
        weight = point_ref[3:4, lanes] * norm_scale
        flux = weight * density * (vel_x * cos_p + vel_y * sin_p)
        push = weight * pressure
        for at, row in enumerate(
            (
                cos_p,
                sin_p,
                point_ref[2:3, lanes],
                flux,
                push * cos_p + flux * vel_x,
                push * sin_p + flux * vel_y,
                flux * vel_z,
            )
        ):
            rows[at, :, lanes] = jnp.broadcast_to(row, (8, width))

    group = 4
    tile = 128 * group
    lane = lax.broadcasted_iota(jnp.int32, (8, 128), 1)

    def add_up(terms):
        while len(terms) > 1:
            terms = [a + b for a, b in zip(terms[0::2], terms[1::2])]
        return terms[0]

    def observers(g, carry):
        at = pl.ds(pl.multiple_of(g * 8, 8), 8)
        obs_x, obs_y, obs_z = obs_x_ref[at, :], obs_y_ref[at, :], obs_z_ref[at, :]
        for part in range(points // tile):
            state = []
            for u in range(group):
                lanes = slice(part * tile + u * 128, part * tile + (u + 1) * 128)
                dx = obs_x - rows[0, :, lanes]
                dy = obs_y - rows[1, :, lanes]
                dz = obs_z - rows[2, :, lanes]
                square = dx * dx + dy * dy + dz * dz
                inverse = lax.rsqrt(square)
                rough = square * inverse
                half = 0.5 * inverse
                dist = rough + half * (square - rough * rough)
                inverse = inverse + inverse * (0.5 - half * (square * inverse))
                along = dx * rows[4, :, lanes] + dy * rows[5, :, lanes] + dz * rows[6, :, lanes]
                amp = inverse * (rows[3, :, lanes] + inverse * along)
                c1, s1 = sincos(dist * omega_base)
                c2, s2 = c1 * c1 - s1 * s1, 2.0 * c1 * s1
                c4, s4 = c2 * c2 - s2 * s2, 2.0 * c2 * s2
                c8, s8 = c4 * c4 - s4 * s4, 2.0 * c4 * s4
                c16, s16 = c8 * c8 - s8 * s8, 2.0 * c8 * s8
                c24 = c16 * c8 - s16 * s8
                state.append(
                    [amp, jnp.zeros_like(amp), amp * c1, amp * s1, 2.0 * c1, 2.0 * c8, 2.0 * c16, 2.0 * c24]
                )

            def put(column, terms):
                total = add_up(terms)
                if part > 0:
                    total = total + acc[column]
                acc[column] = total

            put(8 * BASIS, [one[0] for one in state])
            for n in range(BASIS):
                for trig in range(2):
                    now = [one[2 + trig] for one in state]
                    put(4 * BASIS * trig + n, now)
                    for multiple in range(3):
                        put(
                            4 * BASIS * trig + BASIS * (multiple + 1) + n,
                            [value * one[5 + multiple] for value, one in zip(now, state)],
                        )
                for one in state:
                    c_next = one[4] * one[2] - one[0]
                    s_next = one[4] * one[3] - one[1]
                    one[0], one[1], one[2], one[3] = one[2], one[3], c_next, s_next
        result = jnp.zeros((8, 128), F32)
        for column in range(8 * BASIS + 1):
            result = jnp.where(lane == column, jnp.sum(acc[column], axis=1, keepdims=True), result)
        sums_ref[at, :] = result
        return carry

    lax.fori_loop(0, obs_x_ref.shape[0] // 8, observers, 0)


def expansion():
    spread = np.zeros((24, 768), np.float32)
    for q in range(512):
        spread[q // 64, q] = 1.0
    for lane in range(128):
        spread[8 + (lane // 8) % 8, 512 + lane] = 1.0
        spread[16 + lane % 8, 640 + lane] = 1.0
    return np.concatenate([spread] * 3, axis=0)


def recombination():
    rows = np.zeros((128, 64), np.float32)
    cos_of, sin_of = {}, {}
    unit = np.eye(128, dtype=np.float32)
    cos_of[0], sin_of[0] = unit[8 * BASIS], np.zeros(128, np.float32)
    for n in range(1, BASIS + 1):
        cos_of[n], sin_of[n] = unit[n - 1], unit[4 * BASIS + n - 1]
    for multiple in (1, 2, 3):
        m = multiple * BASIS
        for n in range(1, BASIS + 1):
            cos_of[m + n] = unit[multiple * BASIS + n - 1] - cos_of[m - n]
            sin_of[m + n] = unit[4 * BASIS + multiple * BASIS + n - 1] + sin_of[m - n]
    for k in range(32):
        rows[:, k] = cos_of[k + 1]
        rows[:, 32 + k] = sin_of[k + 1]
    return rows


def on_device(
    element_fields,
    ref_coords,
    local_element,
    owner,
    point_angle,
    point_axial,
    panel_weight,
    obs_radius,
    obs_angle,
    obs_axial,
    step_phase,
    observer_slot,
    prior_spectra,
):
    devices = lax.axis_size(AXES)
    points = local_element.shape[0]
    cap = 4 * points // devices
    observers = obs_radius.shape[0]
    harmonics = step_phase.shape[0]
    norm_scale = 1.0 / math.sqrt(points * devices)
    target = owner.reshape(1, points)

    send, rank = pl.pallas_call(
        functools.partial(pack_kernel, devices, cap),
        out_shape=(
            jax.ShapeDtypeStruct((devices, 4, cap), F32),
            jax.ShapeDtypeStruct((1, points), jnp.int32),
        ),
        name="pack",
    )(target, local_element.reshape(1, points), ref_coords)
    recv = lax.all_to_all(send, AXES, split_axis=0, concat_axis=0, tiled=True)
    ids = recv[:, 0, :].reshape(devices * cap).astype(jnp.int32)
    vmem = pl.BlockSpec(memory_space=pltpu.VMEM)
    served = pl.pallas_call(
        interp_kernel,
        out_shape=jax.ShapeDtypeStruct((devices, FIELDS, cap), F32),
        in_specs=[pl.BlockSpec(memory_space=pltpu.SMEM), vmem, vmem, vmem],
        out_specs=vmem,
        scratch_shapes=[
            pltpu.VMEM((element_fields.shape[0], 8, 512), F32),
            pltpu.VMEM((max(1, cap // 128), min(cap, 128), 512), F32),
        ],
        name="interp",
    )(ids, recv, jnp.asarray(expansion(), BF16), element_fields)
    replies = lax.all_to_all(served, AXES, split_axis=0, concat_axis=0, tiled=True)

    chosen = observer_slot[:, None] == jnp.arange(observers, dtype=jnp.int32)[None, :]
    in_order = lambda x: jnp.sum(jnp.where(chosen, x[:, None], 0.0), axis=0)
    radius = in_order(obs_radius)
    obs_x = in_order(obs_radius * jnp.cos(obs_angle))
    obs_y = in_order(obs_radius * jnp.sin(obs_angle))
    obs_z = in_order(obs_axial)
    spread = lambda x: jnp.broadcast_to(x[:, None], (observers, 128))
    point_rows = jnp.stack([jnp.cos(point_angle), jnp.sin(point_angle), point_axial, panel_weight])
    surface_values, sums = pl.pallas_call(
        functools.partial(spectra_kernel, norm_scale),
        out_shape=(
            jax.ShapeDtypeStruct((FIELDS, points), F32),
            jax.ShapeDtypeStruct((observers, 128), F32),
        ),
        scratch_shapes=[
            pltpu.VMEM((7, 8, points), F32),
            pltpu.VMEM((8 * BASIS + 1, 8, 128), F32),
        ],
        name="spectra",
    )(replies, target, rank, point_rows, spread(obs_x), spread(obs_y), spread(obs_z))

    own = observers // devices
    gathered = lax.all_to_all(sums, AXES, split_axis=0, concat_axis=0, tiled=True)
    summed = jnp.sum(gathered.reshape(devices, own, 128), axis=0)
    me = lax.axis_index(AXES)
    own_radius = lax.dynamic_slice(radius, (me * own,), (own,))
    recombined = jnp.dot(
        summed * own_radius[:, None], jnp.asarray(recombination()), precision=lax.Precision.HIGHEST
    )
    cos_sum, sin_sum = recombined[:, :harmonics].T, recombined[:, harmonics:].T
    cos_f, sin_f = jnp.cos(step_phase)[:, None], jnp.sin(step_phase)[:, None]
    terms = jnp.stack([cos_f * cos_sum - sin_f * sin_sum, -(sin_f * cos_sum + cos_f * sin_sum)])
    return (surface_values, prior_spectra + terms)


def solution(mesh):
    return jax.shard_map(
        on_device,
        mesh=mesh,
        in_specs=(
            P(AXES, None, None),
            P(None, AXES),
            P(AXES),
            P(AXES, None),
            P(AXES),
            P(AXES),
            P(AXES),
            P(),
            P(),
            P(),
            P(),
            P(),
            P(None, None, AXES),
        ),
        out_specs=(P(None, AXES), P(None, None, AXES)),
        check_vma=False,
    )
```

```python
import functools
import math

import jax
import jax.numpy as jnp
import numpy as np
from jax import lax
from jax.experimental import pallas as pl
from jax.experimental.pallas import tpu as pltpu
from jax.sharding import PartitionSpec as P

FIELDS = 5
AXES = ("gx", "gy")
F32 = jnp.float32
BF16 = jnp.bfloat16
BASIS = 8

gll_nodes = np.array(
    [
        -1.0,
        -0.8717401485096066,
        -0.5917001814331423,
        -0.2092992179024789,
        0.2092992179024789,
        0.5917001814331423,
        0.8717401485096066,
        1.0,
    ]
)
gll_scale = np.array(
    [1.0 / np.prod([gll_nodes[i] - gll_nodes[m] for m in range(8) if m != i]) for i in range(8)]
)
omega_base = 0.25


def three_parts(x):
    high = x.astype(BF16)
    rest = x - high.astype(F32)
    middle = rest.astype(BF16)
    low = (rest - middle.astype(F32)).astype(BF16)
    return high, middle, low


def contract_last(a, b):
    return lax.dot_general(a, b, (((1,), (1,)), ((), ())), preferred_element_type=F32)


def where_am_i():
    return lax.axis_index(AXES)


def place_of(device):
    inner = lax.axis_size("gy")
    return (device // inner, lax.rem(device, inner))


def greet(devices):
    me = where_am_i()
    barrier = pltpu.get_barrier_semaphore()

    def signal(step, carry):
        other = lax.rem(me + step, devices)
        pl.semaphore_signal(
            barrier, inc=1, device_id=place_of(other), device_id_type=pl.DeviceIdType.MESH
        )
        return carry

    lax.fori_loop(1, devices, signal, 0)


def met(devices):
    pl.semaphore_wait(pltpu.get_barrier_semaphore(), devices - 1)


def transfer(stage, landing, send_sems, recv_sems, other, sender):
    return pltpu.make_async_remote_copy(
        src_ref=stage.at[other],
        dst_ref=landing.at[sender],
        send_sem=send_sems.at[other],
        recv_sem=recv_sems.at[sender],
        device_id=place_of(other),
        device_id_type=pl.DeviceIdType.MESH,
    )


def finish(devices, stage, landing, send_sems, recv_sems):
    me = where_am_i()

    def wait(step, carry):
        other = lax.rem(me + step, devices)
        transfer(stage, landing, send_sems, recv_sems, other, me).wait_send()
        transfer(stage, landing, send_sems, recv_sems, other, other).wait_recv()
        return carry

    lax.fori_loop(1, devices, wait, 0)


def pack_kernel(
    devices,
    cap,
    target_ref,
    ids_ref,
    coords_ref,
    recv_ref,
    served_ids_ref,
    rank_ref,
    send_ref,
    landing,
    send_sems,
    recv_sems,
):
    greet(devices)
    me = where_am_i()
    points = target_ref.shape[1]
    width = math.gcd(points, 512)
    before = (
        lax.broadcasted_iota(jnp.int32, (width, width), 0)
        < lax.broadcasted_iota(jnp.int32, (width, width), 1)
    )
    before = jnp.where(before, 1.0, 0.0).astype(BF16)
    offset = jnp.zeros((devices, 1), F32)
    sums = [jnp.zeros((devices, cap), F32) for _ in range(4)]
    for block in range(points // width):
        lanes = slice(block * width, (block + 1) * width)
        mine = target_ref[:, lanes] == lax.broadcasted_iota(jnp.int32, (devices, width), 0)
        hot = jnp.where(mine, 1.0, 0.0)
        hot_half = hot.astype(BF16)
        within = jnp.dot(hot_half, before, preferred_element_type=F32) + offset
        rank = jnp.sum(hot * within, axis=0, keepdims=True).astype(jnp.int32)
        offset = offset + jnp.sum(hot, axis=1, keepdims=True)
        rank_ref[:, lanes] = rank
        spot = jnp.where(lax.broadcasted_iota(jnp.int32, (cap, width), 0) == rank, 1.0, 0.0)
        spot = spot.astype(BF16)
        for entry in range(4):
            if entry == 0:
                row = ids_ref[:, lanes].astype(F32)
            else:
                row = coords_ref[entry - 1 : entry, lanes]
            for part in three_parts(row * hot):
                sums[entry] = sums[entry] + contract_last(part, spot)
    for entry in range(4):
        send_ref[:, entry, :] = sums[entry]
    met(devices)

    def begin(step, carry):
        other = lax.rem(me + step, devices)
        transfer(send_ref, landing, send_sems, recv_sems, other, me).start()
        return carry

    lax.fori_loop(1, devices, begin, 0)
    landing[me] = send_ref[me]
    finish(devices, send_ref, landing, send_sems, recv_sems)
    recv_ref[...] = landing[...]
    served_ids_ref[...] = landing[:, 0, :].astype(jnp.int32)


def interp_kernel(
    ids_ref,
    recv_ref,
    expand_ref,
    fields_ref,
    out_ref,
    table,
    weights_even,
    weights_odd,
    stage,
    landing,
    send_sems,
    recv_sems,
):
    devices, _, cap = recv_ref.shape
    greet(devices)
    me = where_am_i()
    block = min(cap, 128)
    elements = fields_ref.shape[1]
    chunk = math.gcd(elements, 16)

    def widen(step, carry):
        rows = pl.ds(pl.multiple_of(step * chunk, chunk), chunk)
        for f in range(FIELDS):
            table[rows, f, :] = fields_ref[f, rows, :].astype(F32)
        return carry

    lax.fori_loop(0, elements // chunk, widen, 0)
    node = lax.broadcasted_iota(jnp.int32, (8, block), 0)
    lane = lax.broadcasted_iota(jnp.int32, (FIELDS, block), 1)
    scale = jnp.zeros((8, block), F32)
    for i in range(8):
        scale = jnp.where(node == i, float(gll_scale[i]), scale)

    def fill(weights, s):
        for half in range(cap // block):
            lanes = slice(half * block, (half + 1) * block)
            bases = []
            for axis in range(3):
                x = recv_ref[s, axis + 1 : axis + 2, lanes]
                product = scale
                for m in range(8):
                    product = product * jnp.where(node == m, 1.0, x - float(gll_nodes[m]))
                bases.append(product)
            stacked = jnp.concatenate(bases, axis=0)
            parts = jnp.concatenate([p.astype(F32) for p in three_parts(stacked)], axis=0)
            parts = parts.T.astype(BF16)
            wide = jnp.dot(parts, expand_ref[...], preferred_element_type=F32)
            pair = wide[:, 512:640] * wide[:, 640:768]
            for quarter in range(4):
                columns = slice(quarter * 128, (quarter + 1) * 128)
                weights[half, :, columns] = wide[:, columns] * pair

    def evaluate(weights, s):
        for half in range(cap // block):
            lanes = slice(half * block, (half + 1) * block)
            result = jnp.zeros((FIELDS, block), F32)
            for p in range(block):
                e = ids_ref[s, half * block + p]
                total = None
                for quarter in range(4):
                    columns = slice(quarter * 128, (quarter + 1) * 128)
                    term = table[e, 0:FIELDS, columns] * weights[half, p : p + 1, columns]
                    total = term if total is None else total + term
                value = jnp.sum(total, axis=1, keepdims=True)
                result = jnp.where(lane == p, value, result)
            stage[s, :, lanes] = result

    def at_step(step):
        return lax.rem(me + 1 + step, devices)

    fill(weights_even, at_step(0))
    met(devices)

    def two_sources(pair_step, carry):
        first, second = at_step(2 * pair_step), at_step(2 * pair_step + 1)
        third = at_step(2 * pair_step + 2)
        fill(weights_odd, second)
        evaluate(weights_even, first)
        transfer(stage, landing, send_sems, recv_sems, first, me).start()
        fill(weights_even, third)
        evaluate(weights_odd, second)

        @pl.when(2 * pair_step + 1 < devices - 1)
        def _():
            transfer(stage, landing, send_sems, recv_sems, second, me).start()

        return carry

    lax.fori_loop(0, devices // 2, two_sources, 0)
    landing[me] = stage[me]
    finish(devices, stage, landing, send_sems, recv_sems)
    out_ref[...] = landing[...]


def sincos(angle):
    turns = jnp.floor(angle * float(2.0 / math.pi) + 0.5)
    r = angle - turns * 1.5703125
    r = r - turns * 4.837512969970703125e-4
    r = r - turns * 7.54978995489188e-8
    z = r * r
    sine = ((-1.9515295891e-4 * z + 8.3321608736e-3) * z - 1.6666654611e-1) * z * r + r
    cosine = (
        (2.443315711809948e-5 * z - 1.388731625493765e-3) * z + 4.166664568298827e-2
    ) * z * z + (1.0 - 0.5 * z)
    quadrant = turns.astype(jnp.int32)
    odd = (quadrant & 1) == 1
    first = jnp.where(odd, sine, cosine)
    second = jnp.where(odd, cosine, sine)
    first = jnp.where(((quadrant + 1) & 2) == 2, -first, first)
    second = jnp.where((quadrant & 2) == 2, -second, second)
    return first, second


def spectra_kernel(
    norm_scale,
    replies_ref,
    target_ref,
    rank_ref,
    point_ref,
    obs_ref,
    slot_ref,
    surface_ref,
    sums_ref,
    rows,
    acc,
    stage,
    landing,
    send_sems,
    recv_sems,
):
    devices, _, cap = replies_ref.shape
    greet(devices)
    me = where_am_i()
    points = target_ref.shape[1]
    width = math.gcd(points, 512)
    parts = [three_parts(replies_ref[:, f, :]) for f in range(FIELDS)]
    stacked = jnp.concatenate([p for triple in parts for p in triple], axis=0)
    for block in range(points // width):
        lanes = slice(block * width, (block + 1) * width)
        mine = target_ref[:, lanes] == lax.broadcasted_iota(jnp.int32, (devices, width), 0)
        spot = jnp.where(
            lax.broadcasted_iota(jnp.int32, (cap, width), 0) == rank_ref[:, lanes], 1.0, 0.0
        ).astype(BF16)
        found = jnp.dot(stacked, spot, preferred_element_type=F32)
        found = found.reshape(FIELDS, 3, devices, width)
        values = []
        for f in range(FIELDS):
            whole = (found[f, 0] + found[f, 1]) + found[f, 2]
            value = jnp.sum(jnp.where(mine, whole, 0.0), axis=0, keepdims=True)
            surface_ref[f : f + 1, lanes] = value
            values.append(value)
        density, vel_x, vel_y, vel_z, pressure = values
        cos_p, sin_p = sincos(point_ref[0:1, lanes])
        weight = point_ref[2:3, lanes] * norm_scale
        flux = weight * density * (vel_x * cos_p + vel_y * sin_p)
        push = weight * pressure
        for at, row in enumerate(
            (
                cos_p,
                sin_p,
                point_ref[1:2, lanes],
                flux,
                push * cos_p + flux * vel_x,
                push * sin_p + flux * vel_y,
                flux * vel_z,
            )
        ):
            rows[at, :, lanes] = jnp.broadcast_to(row, (8, width))

    group = 4
    tile = 128 * group
    lane = lax.broadcasted_iota(jnp.int32, (8, 128), 1)

    def add_up(terms):
        while len(terms) > 1:
            terms = [a + b for a, b in zip(terms[0::2], terms[1::2])]
        return terms[0]

    count = obs_ref.shape[1]
    groups, own = count // 8, stage.shape[1]
    per_group = 8 // own
    met(devices)

    def observers(step, carry):
        g = lax.rem(me // per_group + 1 + step, groups)
        column_of = lax.broadcasted_iota(jnp.int32, (8, count), 0) + g * 8
        chosen = slot_ref[...] == column_of
        spread = [
            jnp.broadcast_to(
                jnp.sum(jnp.where(chosen, obs_ref[i : i + 1, :], 0.0), axis=1, keepdims=True),
                (8, 128),
            )
            for i in range(4)
        ]
        obs_x, obs_y, obs_z, radius = spread
        for part in range(points // tile):
            state = []
            for u in range(group):
                lanes = slice(part * tile + u * 128, part * tile + (u + 1) * 128)
                dx = obs_x - rows[0, :, lanes]
                dy = obs_y - rows[1, :, lanes]
                dz = obs_z - rows[2, :, lanes]
                square = dx * dx + dy * dy + dz * dz
                inverse = lax.rsqrt(square)
                rough = square * inverse
                half = 0.5 * inverse
                dist = rough + half * (square - rough * rough)
                inverse = inverse + inverse * (0.5 - half * (square * inverse))
                along = dx * rows[4, :, lanes] + dy * rows[5, :, lanes] + dz * rows[6, :, lanes]
                amp = inverse * (rows[3, :, lanes] + inverse * along)
                c1, s1 = sincos(dist * omega_base)
                c2, s2 = c1 * c1 - s1 * s1, 2.0 * c1 * s1
                c4, s4 = c2 * c2 - s2 * s2, 2.0 * c2 * s2
                c8, s8 = c4 * c4 - s4 * s4, 2.0 * c4 * s4
                c16, s16 = c8 * c8 - s8 * s8, 2.0 * c8 * s8
                c24 = c16 * c8 - s16 * s8
                state.append(
                    [amp, jnp.zeros_like(amp), amp * c1, amp * s1, 2.0 * c1, 2.0 * c8, 2.0 * c16, 2.0 * c24]
                )

            def put(column, terms):
                total = add_up(terms)
                if part > 0:
                    total = total + acc[column]
                acc[column] = total

            put(8 * BASIS, [one[0] for one in state])
            for n in range(BASIS):
                for trig in range(2):
                    now = [one[2 + trig] for one in state]
                    put(4 * BASIS * trig + n, now)
                    for multiple in range(3):
                        put(
                            4 * BASIS * trig + BASIS * (multiple + 1) + n,
                            [value * one[5 + multiple] for value, one in zip(now, state)],
                        )
                for one in state:
                    c_next = one[4] * one[2] - one[0]
                    s_next = one[4] * one[3] - one[1]
                    one[0], one[1], one[2], one[3] = one[2], one[3], c_next, s_next
        result = jnp.zeros((8, 128), F32)
        for column in range(8 * BASIS + 1):
            result = jnp.where(lane == column, jnp.sum(acc[column], axis=1, keepdims=True), result)
        result = result * radius
        for j in range(per_group):
            other = g * per_group + j
            stage[other] = result[j * own : (j + 1) * own, :]

            @pl.when(other != me)
            def _():
                transfer(stage, landing, send_sems, recv_sems, other, me).start()

        return carry

    lax.fori_loop(0, groups, observers, 0)
    landing[me] = stage[me]
    finish(devices, stage, landing, send_sems, recv_sems)
    sums_ref[...] = jnp.sum(landing[...], axis=0)


def expansion():
    spread = np.zeros((24, 768), np.float32)
    for q in range(512):
        spread[q // 64, q] = 1.0
    for lane in range(128):
        spread[8 + (lane // 8) % 8, 512 + lane] = 1.0
        spread[16 + lane % 8, 640 + lane] = 1.0
    return np.concatenate([spread] * 3, axis=0)


def recombination():
    rows = np.zeros((128, 64), np.float32)
    cos_of, sin_of = {}, {}
    unit = np.eye(128, dtype=np.float32)
    cos_of[0], sin_of[0] = unit[8 * BASIS], np.zeros(128, np.float32)
    for n in range(1, BASIS + 1):
        cos_of[n], sin_of[n] = unit[n - 1], unit[4 * BASIS + n - 1]
    for multiple in (1, 2, 3):
        m = multiple * BASIS
        for n in range(1, BASIS + 1):
            cos_of[m + n] = unit[multiple * BASIS + n - 1] - cos_of[m - n]
            sin_of[m + n] = unit[4 * BASIS + multiple * BASIS + n - 1] + sin_of[m - n]
    for k in range(32):
        rows[:, k] = cos_of[k + 1]
        rows[:, 32 + k] = sin_of[k + 1]
    return rows


def on_device(
    element_fields,
    ref_coords,
    local_element,
    owner,
    point_angle,
    point_axial,
    panel_weight,
    obs_radius,
    obs_angle,
    obs_axial,
    step_phase,
    observer_slot,
    prior_spectra,
):
    devices = lax.axis_size(AXES)
    points = local_element.shape[0]
    cap = 4 * points // devices
    observers = obs_radius.shape[0]
    harmonics = step_phase.shape[0]
    norm_scale = 1.0 / math.sqrt(points * devices)
    target = owner.reshape(1, points)

    own = observers // devices
    vmem = pl.BlockSpec(memory_space=pltpu.VMEM)
    sems = [pltpu.SemaphoreType.DMA((devices,)), pltpu.SemaphoreType.DMA((devices,))]

    def params(number):
        return pltpu.CompilerParams(collective_id=number, has_side_effects=True)

    recv, ids, rank = pl.pallas_call(
        functools.partial(pack_kernel, devices, cap),
        out_shape=(
            jax.ShapeDtypeStruct((devices, 4, cap), F32),
            jax.ShapeDtypeStruct((devices, cap), jnp.int32),
            jax.ShapeDtypeStruct((1, points), jnp.int32),
        ),
        scratch_shapes=[pltpu.VMEM((devices, 4, cap), F32), pltpu.VMEM((devices, 4, cap), F32)] + sems,
        compiler_params=params(0),
        name="pack",
    )(target, local_element.reshape(1, points), ref_coords)
    half_shape = (max(1, cap // 128), min(cap, 128), 512)
    replies = pl.pallas_call(
        interp_kernel,
        out_shape=jax.ShapeDtypeStruct((devices, FIELDS, cap), F32),
        in_specs=[pl.BlockSpec(memory_space=pltpu.SMEM), vmem, vmem, vmem],
        out_specs=vmem,
        scratch_shapes=[
            pltpu.VMEM((element_fields.shape[0], 8, 512), F32),
            pltpu.VMEM(half_shape, F32),
            pltpu.VMEM(half_shape, F32),
            pltpu.VMEM((devices, FIELDS, cap), F32),
            pltpu.VMEM((devices, FIELDS, cap), F32),
        ]
        + sems,
        compiler_params=params(1),
        name="interp",
    )(ids, recv, jnp.asarray(expansion(), BF16), element_fields.transpose(1, 0, 2))

    obs_rows = jnp.stack(
        [obs_radius * jnp.cos(obs_angle), obs_radius * jnp.sin(obs_angle), obs_axial, obs_radius]
    )
    surface_values, summed = pl.pallas_call(
        functools.partial(spectra_kernel, norm_scale),
        out_shape=(
            jax.ShapeDtypeStruct((FIELDS, points), F32),
            jax.ShapeDtypeStruct((own, 128), F32),
        ),
        scratch_shapes=[
            pltpu.VMEM((7, 8, points), F32),
            pltpu.VMEM((8 * BASIS + 1, 8, 128), F32),
            pltpu.VMEM((devices, own, 128), F32),
            pltpu.VMEM((devices, own, 128), F32),
        ]
        + sems,
        compiler_params=params(2),
        name="spectra",
    )(
        replies,
        target,
        rank,
        jnp.stack([point_angle, point_axial, panel_weight]),
        obs_rows,
        observer_slot.reshape(1, observers),
    )
    recombined = jnp.dot(
        summed, jnp.asarray(recombination()), precision=lax.Precision.HIGHEST
    )
    cos_sum, sin_sum = recombined[:, :harmonics].T, recombined[:, harmonics:].T
    cos_f, sin_f = jnp.cos(step_phase)[:, None], jnp.sin(step_phase)[:, None]
    terms = jnp.stack([cos_f * cos_sum - sin_f * sin_sum, -(sin_f * cos_sum + cos_f * sin_sum)])
    return (surface_values, prior_spectra + terms)


def solution(mesh):
    return jax.shard_map(
        on_device,
        mesh=mesh,
        in_specs=(
            P(AXES, None, None),
            P(None, AXES),
            P(AXES),
            P(AXES, None),
            P(AXES),
            P(AXES),
            P(AXES),
            P(),
            P(),
            P(),
            P(),
            P(),
            P(None, None, AXES),
        ),
        out_specs=(P(None, AXES), P(None, None, AXES)),
        check_vma=False,
    )
```

```python
import functools
import math

import jax
import jax.numpy as jnp
import numpy as np
from jax import lax
from jax.experimental import pallas as pl
from jax.experimental.pallas import tpu as pltpu
from jax.sharding import PartitionSpec as P

FIELDS = 5
AXES = ("gx", "gy")
F32 = jnp.float32
BF16 = jnp.bfloat16
BASIS = 8

gll_nodes = np.array(
    [
        -1.0,
        -0.8717401485096066,
        -0.5917001814331423,
        -0.2092992179024789,
        0.2092992179024789,
        0.5917001814331423,
        0.8717401485096066,
        1.0,
    ]
)
gll_scale = np.array(
    [1.0 / np.prod([gll_nodes[i] - gll_nodes[m] for m in range(8) if m != i]) for i in range(8)]
)
omega_base = 0.25


def three_parts(x):
    high = x.astype(BF16)
    rest = x - high.astype(F32)
    middle = rest.astype(BF16)
    low = (rest - middle.astype(F32)).astype(BF16)
    return high, middle, low


def contract_last(a, b):
    return lax.dot_general(a, b, (((1,), (1,)), ((), ())), preferred_element_type=F32)


def where_am_i():
    return lax.axis_index(AXES)


def place_of(device):
    inner = lax.axis_size("gy")
    return (device // inner, lax.rem(device, inner))


def greet(devices):
    me = where_am_i()
    barrier = pltpu.get_barrier_semaphore()

    def signal(step, carry):
        other = lax.rem(me + step, devices)
        pl.semaphore_signal(
            barrier, inc=1, device_id=place_of(other), device_id_type=pl.DeviceIdType.MESH
        )
        return carry

    lax.fori_loop(1, devices, signal, 0)


def met(devices):
    pl.semaphore_wait(pltpu.get_barrier_semaphore(), devices - 1)


def transfer(stage, landing, send_sems, recv_sems, other, sender):
    return pltpu.make_async_remote_copy(
        src_ref=stage.at[other],
        dst_ref=landing.at[sender],
        send_sem=send_sems.at[other],
        recv_sem=recv_sems.at[sender],
        device_id=place_of(other),
        device_id_type=pl.DeviceIdType.MESH,
    )


def finish(devices, stage, landing, send_sems, recv_sems):
    me = where_am_i()

    def wait(step, carry):
        other = lax.rem(me + step, devices)
        transfer(stage, landing, send_sems, recv_sems, other, me).wait_send()
        transfer(stage, landing, send_sems, recv_sems, other, other).wait_recv()
        return carry

    lax.fori_loop(1, devices, wait, 0)


def pack_kernel(
    devices,
    cap,
    target_ref,
    ids_ref,
    coords_ref,
    recv_ref,
    served_ids_ref,
    rank_ref,
    send_ref,
    landing,
    send_sems,
    recv_sems,
):
    greet(devices)
    me = where_am_i()
    points = target_ref.shape[1]
    width = math.gcd(points, 512)
    before = (
        lax.broadcasted_iota(jnp.int32, (width, width), 0)
        < lax.broadcasted_iota(jnp.int32, (width, width), 1)
    )
    before = jnp.where(before, 1.0, 0.0).astype(BF16)
    offset = jnp.zeros((devices, 1), F32)
    sums = [jnp.zeros((devices, cap), F32) for _ in range(4)]
    for block in range(points // width):
        lanes = slice(block * width, (block + 1) * width)
        mine = target_ref[:, lanes] == lax.broadcasted_iota(jnp.int32, (devices, width), 0)
        hot = jnp.where(mine, 1.0, 0.0)
        hot_half = hot.astype(BF16)
        within = jnp.dot(hot_half, before, preferred_element_type=F32) + offset
        rank = jnp.sum(hot * within, axis=0, keepdims=True).astype(jnp.int32)
        offset = offset + jnp.sum(hot, axis=1, keepdims=True)
        rank_ref[:, lanes] = rank
        spot = jnp.where(lax.broadcasted_iota(jnp.int32, (cap, width), 0) == rank, 1.0, 0.0)
        spot = spot.astype(BF16)
        for entry in range(4):
            if entry == 0:
                row = ids_ref[:, lanes].astype(F32)
            else:
                row = coords_ref[entry - 1 : entry, lanes]
            for part in three_parts(row * hot):
                sums[entry] = sums[entry] + contract_last(part, spot)
    for entry in range(4):
        send_ref[:, entry, :] = sums[entry]
    met(devices)

    def begin(step, carry):
        other = lax.rem(me + step, devices)
        transfer(send_ref, landing, send_sems, recv_sems, other, me).start()
        return carry

    lax.fori_loop(1, devices, begin, 0)
    landing[me] = send_ref[me]
    finish(devices, send_ref, landing, send_sems, recv_sems)
    recv_ref[...] = landing[...]
    served_ids_ref[...] = landing[:, 0, :].astype(jnp.int32)


def interp_kernel(
    ids_ref,
    recv_ref,
    expand_ref,
    fields_ref,
    out_ref,
    table,
    weights_even,
    weights_odd,
    stage,
    landing,
    send_sems,
    recv_sems,
):
    devices, _, cap = recv_ref.shape
    greet(devices)
    me = where_am_i()
    block = min(cap, 128)
    elements = fields_ref.shape[1]
    chunk = math.gcd(elements, 16)

    def widen(step, carry):
        rows = pl.ds(pl.multiple_of(step * chunk, chunk), chunk)
        for f in range(FIELDS):
            table[rows, f, :] = fields_ref[f, rows, :].astype(F32)
        return carry

    lax.fori_loop(0, elements // chunk, widen, 0)
    node = lax.broadcasted_iota(jnp.int32, (8, block), 0)
    lane = lax.broadcasted_iota(jnp.int32, (FIELDS, block), 1)
    scale = jnp.zeros((8, block), F32)
    for i in range(8):
        scale = jnp.where(node == i, float(gll_scale[i]), scale)

    def fill(weights, s):
        for half in range(cap // block):
            lanes = slice(half * block, (half + 1) * block)
            bases = []
            for axis in range(3):
                x = recv_ref[s, axis + 1 : axis + 2, lanes]
                product = scale
                for m in range(8):
                    product = product * jnp.where(node == m, 1.0, x - float(gll_nodes[m]))
                bases.append(product)
            stacked = jnp.concatenate(bases, axis=0)
            parts = jnp.concatenate([p.astype(F32) for p in three_parts(stacked)], axis=0)
            parts = parts.T.astype(BF16)
            wide = jnp.dot(parts, expand_ref[...], preferred_element_type=F32)
            pair = wide[:, 512:640] * wide[:, 640:768]
            for quarter in range(4):
                columns = slice(quarter * 128, (quarter + 1) * 128)
                weights[half, :, columns] = wide[:, columns] * pair

    def evaluate(weights, s):
        for half in range(cap // block):
            lanes = slice(half * block, (half + 1) * block)
            result = jnp.zeros((FIELDS, block), F32)
            for p in range(block):
                e = ids_ref[s, half * block + p]
                total = None
                for quarter in range(4):
                    columns = slice(quarter * 128, (quarter + 1) * 128)
                    term = table[e, 0:FIELDS, columns] * weights[half, p : p + 1, columns]
                    total = term if total is None else total + term
                value = jnp.sum(total, axis=1, keepdims=True)
                result = jnp.where(lane == p, value, result)
            stage[s, :, lanes] = result

    def at_step(step):
        return lax.rem(me + 1 + step, devices)

    fill(weights_even, at_step(0))
    met(devices)

    def two_sources(pair_step, carry):
        first, second = at_step(2 * pair_step), at_step(2 * pair_step + 1)
        third = at_step(2 * pair_step + 2)
        fill(weights_odd, second)
        evaluate(weights_even, first)
        transfer(stage, landing, send_sems, recv_sems, first, me).start()
        fill(weights_even, third)
        evaluate(weights_odd, second)

        @pl.when(2 * pair_step + 1 < devices - 1)
        def _():
            transfer(stage, landing, send_sems, recv_sems, second, me).start()

        return carry

    lax.fori_loop(0, devices // 2, two_sources, 0)
    landing[me] = stage[me]
    finish(devices, stage, landing, send_sems, recv_sems)
    out_ref[...] = landing[...]


def sincos(angle):
    turns = jnp.floor(angle * float(2.0 / math.pi) + 0.5)
    r = angle - turns * 1.5703125
    r = r - turns * 4.837512969970703125e-4
    r = r - turns * 7.54978995489188e-8
    z = r * r
    sine = ((-1.9515295891e-4 * z + 8.3321608736e-3) * z - 1.6666654611e-1) * z * r + r
    cosine = (
        (2.443315711809948e-5 * z - 1.388731625493765e-3) * z + 4.166664568298827e-2
    ) * z * z + (1.0 - 0.5 * z)
    quadrant = turns.astype(jnp.int32)
    odd = (quadrant & 1) == 1
    first = jnp.where(odd, sine, cosine)
    second = jnp.where(odd, cosine, sine)
    first = jnp.where(((quadrant + 1) & 2) == 2, -first, first)
    second = jnp.where((quadrant & 2) == 2, -second, second)
    return first, second


def sincos_by_doubling(angle):
    x = angle * 0.125
    z = x * x
    sine = 1.0 / 362880.0 * z - 1.0 / 5040.0
    sine = sine * z + 1.0 / 120.0
    sine = sine * z - 1.0 / 6.0
    sine = (sine * z + 1.0) * x
    cosine = -1.0 / 3628800.0 * z + 1.0 / 40320.0
    cosine = cosine * z - 1.0 / 720.0
    cosine = cosine * z + 1.0 / 24.0
    cosine = cosine * z - 0.5
    cosine = cosine * z + 1.0
    for _ in range(3):
        twice = sine + sine
        cosine, sine = 1.0 - twice * sine, twice * cosine
    return cosine, sine


def spectra_kernel(
    norm_scale,
    replies_ref,
    target_ref,
    rank_ref,
    point_ref,
    obs_ref,
    slot_ref,
    surface_ref,
    sums_ref,
    rows,
    acc,
    observer,
    stage,
    landing,
    send_sems,
    recv_sems,
):
    devices, _, cap = replies_ref.shape
    greet(devices)
    me = where_am_i()
    points = target_ref.shape[1]
    width = math.gcd(points, 512)
    parts = [three_parts(replies_ref[:, f, :]) for f in range(FIELDS)]
    stacked = jnp.concatenate([p for triple in parts for p in triple], axis=0)
    for block in range(points // width):
        lanes = slice(block * width, (block + 1) * width)
        mine = target_ref[:, lanes] == lax.broadcasted_iota(jnp.int32, (devices, width), 0)
        spot = jnp.where(
            lax.broadcasted_iota(jnp.int32, (cap, width), 0) == rank_ref[:, lanes], 1.0, 0.0
        ).astype(BF16)
        found = jnp.dot(stacked, spot, preferred_element_type=F32)
        found = found.reshape(FIELDS, 3, devices, width)
        values = []
        for f in range(FIELDS):
            whole = (found[f, 0] + found[f, 1]) + found[f, 2]
            value = jnp.sum(jnp.where(mine, whole, 0.0), axis=0, keepdims=True)
            surface_ref[f : f + 1, lanes] = value
            values.append(value)
        density, vel_x, vel_y, vel_z, pressure = values
        cos_p, sin_p = sincos(point_ref[0:1, lanes])
        weight = point_ref[2:3, lanes] * norm_scale
        flux = weight * density * (vel_x * cos_p + vel_y * sin_p)
        push = weight * pressure
        for at, row in enumerate(
            (
                cos_p,
                sin_p,
                point_ref[1:2, lanes],
                flux,
                push * cos_p + flux * vel_x,
                push * sin_p + flux * vel_y,
                flux * vel_z,
            )
        ):
            rows[at, :, lanes] = jnp.broadcast_to(row, (8, width))

    group = 4
    tile = 128 * group
    lane = lax.broadcasted_iota(jnp.int32, (8, 128), 1)

    def add_up(terms):
        while len(terms) > 1:
            terms = [a + b for a, b in zip(terms[0::2], terms[1::2])]
        return terms[0]

    count = obs_ref.shape[1]
    groups, own = count // 8, stage.shape[1]
    per_group = 8 // own
    chosen = slot_ref[...] == lax.broadcasted_iota(jnp.int32, (count, count), 0)
    for i in range(4):
        column = jnp.sum(jnp.where(chosen, obs_ref[i : i + 1, :], 0.0), axis=1, keepdims=True)
        observer[i] = jnp.broadcast_to(column, (count, 128))
    met(devices)

    def observers(step, carry):
        g = lax.rem(me // per_group + 1 + step, groups)
        at = pl.ds(pl.multiple_of(g * 8, 8), 8)
        obs_x, obs_y, obs_z = observer[0, at, :], observer[1, at, :], observer[2, at, :]
        for part in range(points // tile):
            state = []
            for u in range(group):
                lanes = slice(part * tile + u * 128, part * tile + (u + 1) * 128)
                dx = obs_x - rows[0, :, lanes]
                dy = obs_y - rows[1, :, lanes]
                dz = obs_z - rows[2, :, lanes]
                square = dx * dx + dy * dy + dz * dz
                inverse = lax.rsqrt(square)
                rough = square * inverse
                half = 0.5 * inverse
                dist = rough + half * (square - rough * rough)
                along = dx * rows[4, :, lanes] + dy * rows[5, :, lanes] + dz * rows[6, :, lanes]
                amp = inverse * (rows[3, :, lanes] + inverse * along)
                c1, s1 = sincos_by_doubling(dist * omega_base)
                t1 = s1 + s1
                c2, s2 = 1.0 - t1 * s1, t1 * c1
                t2 = s2 + s2
                c4, s4 = 1.0 - t2 * s2, t2 * c2
                t4 = s4 + s4
                c8, s8 = 1.0 - t4 * s4, t4 * c4
                t8 = s8 + s8
                c16, s16 = 1.0 - t8 * s8, t8 * c8
                c24 = c16 * c8 - s16 * s8
                state.append(
                    [amp, jnp.zeros_like(amp), amp * c1, amp * s1, 2.0 * c1, 2.0 * c8, 2.0 * c16, 2.0 * c24]
                )

            def put(column, terms):
                total = add_up(terms)
                if part > 0:
                    total = total + acc[column]
                acc[column] = total

            put(8 * BASIS, [one[0] for one in state])
            for n in range(BASIS):
                for trig in range(2):
                    now = [one[2 + trig] for one in state]
                    put(4 * BASIS * trig + n, now)
                    for multiple in range(3):
                        put(
                            4 * BASIS * trig + BASIS * (multiple + 1) + n,
                            [value * one[5 + multiple] for value, one in zip(now, state)],
                        )
                for one in state:
                    c_next = one[4] * one[2] - one[0]
                    s_next = one[4] * one[3] - one[1]
                    one[0], one[1], one[2], one[3] = one[2], one[3], c_next, s_next
        result = jnp.zeros((8, 128), F32)
        for column in range(8 * BASIS + 1):
            result = jnp.where(lane == column, jnp.sum(acc[column], axis=1, keepdims=True), result)
        result = result * observer[3, at, :]
        for j in range(per_group):
            other = g * per_group + j
            stage[other] = result[j * own : (j + 1) * own, :]

            @pl.when(other != me)
            def _():
                transfer(stage, landing, send_sems, recv_sems, other, me).start()

        return carry

    lax.fori_loop(0, groups, observers, 0)
    landing[me] = stage[me]
    finish(devices, stage, landing, send_sems, recv_sems)
    sums_ref[...] = jnp.sum(landing[...], axis=0)


def expansion():
    spread = np.zeros((24, 768), np.float32)
    for q in range(512):
        spread[q // 64, q] = 1.0
    for lane in range(128):
        spread[8 + (lane // 8) % 8, 512 + lane] = 1.0
        spread[16 + lane % 8, 640 + lane] = 1.0
    return np.concatenate([spread] * 3, axis=0)


def recombination():
    rows = np.zeros((128, 64), np.float32)
    cos_of, sin_of = {}, {}
    unit = np.eye(128, dtype=np.float32)
    cos_of[0], sin_of[0] = unit[8 * BASIS], np.zeros(128, np.float32)
    for n in range(1, BASIS + 1):
        cos_of[n], sin_of[n] = unit[n - 1], unit[4 * BASIS + n - 1]
    for multiple in (1, 2, 3):
        m = multiple * BASIS
        for n in range(1, BASIS + 1):
            cos_of[m + n] = unit[multiple * BASIS + n - 1] - cos_of[m - n]
            sin_of[m + n] = unit[4 * BASIS + multiple * BASIS + n - 1] + sin_of[m - n]
    for k in range(32):
        rows[:, k] = cos_of[k + 1]
        rows[:, 32 + k] = sin_of[k + 1]
    return rows


def on_device(
    element_fields,
    ref_coords,
    local_element,
    owner,
    point_angle,
    point_axial,
    panel_weight,
    obs_radius,
    obs_angle,
    obs_axial,
    step_phase,
    observer_slot,
    prior_spectra,
):
    devices = lax.axis_size(AXES)
    points = local_element.shape[0]
    cap = 4 * points // devices
    observers = obs_radius.shape[0]
    harmonics = step_phase.shape[0]
    norm_scale = 1.0 / math.sqrt(points * devices)
    target = owner.reshape(1, points)

    own = observers // devices
    vmem = pl.BlockSpec(memory_space=pltpu.VMEM)
    sems = [pltpu.SemaphoreType.DMA((devices,)), pltpu.SemaphoreType.DMA((devices,))]

    def params(number):
        return pltpu.CompilerParams(collective_id=number, has_side_effects=True)

    recv, ids, rank = pl.pallas_call(
        functools.partial(pack_kernel, devices, cap),
        out_shape=(
            jax.ShapeDtypeStruct((devices, 4, cap), F32),
            jax.ShapeDtypeStruct((devices, cap), jnp.int32),
            jax.ShapeDtypeStruct((1, points), jnp.int32),
        ),
        scratch_shapes=[pltpu.VMEM((devices, 4, cap), F32), pltpu.VMEM((devices, 4, cap), F32)] + sems,
        compiler_params=params(0),
        name="pack",
    )(target, local_element.reshape(1, points), ref_coords)
    half_shape = (max(1, cap // 128), min(cap, 128), 512)
    replies = pl.pallas_call(
        interp_kernel,
        out_shape=jax.ShapeDtypeStruct((devices, FIELDS, cap), F32),
        in_specs=[pl.BlockSpec(memory_space=pltpu.SMEM), vmem, vmem, vmem],
        out_specs=vmem,
        scratch_shapes=[
            pltpu.VMEM((element_fields.shape[0], 8, 512), F32),
            pltpu.VMEM(half_shape, F32),
            pltpu.VMEM(half_shape, F32),
            pltpu.VMEM((devices, FIELDS, cap), F32),
            pltpu.VMEM((devices, FIELDS, cap), F32),
        ]
        + sems,
        compiler_params=params(1),
        name="interp",
    )(ids, recv, jnp.asarray(expansion(), BF16), element_fields.transpose(1, 0, 2))

    obs_rows = jnp.stack(
        [obs_radius * jnp.cos(obs_angle), obs_radius * jnp.sin(obs_angle), obs_axial, obs_radius]
    )
    surface_values, summed = pl.pallas_call(
        functools.partial(spectra_kernel, norm_scale),
        out_shape=(
            jax.ShapeDtypeStruct((FIELDS, points), F32),
            jax.ShapeDtypeStruct((own, 128), F32),
        ),
        scratch_shapes=[
            pltpu.VMEM((7, 8, points), F32),
            pltpu.VMEM((8 * BASIS + 1, 8, 128), F32),
            pltpu.VMEM((4, observers, 128), F32),
            pltpu.VMEM((devices, own, 128), F32),
            pltpu.VMEM((devices, own, 128), F32),
        ]
        + sems,
        compiler_params=params(2),
        name="spectra",
    )(
        replies,
        target,
        rank,
        jnp.stack([point_angle, point_axial, panel_weight]),
        obs_rows,
        observer_slot.reshape(1, observers),
    )
    recombined = jnp.dot(
        summed, jnp.asarray(recombination()), precision=lax.Precision.HIGHEST
    )
    cos_sum, sin_sum = recombined[:, :harmonics].T, recombined[:, harmonics:].T
    cos_f, sin_f = jnp.cos(step_phase)[:, None], jnp.sin(step_phase)[:, None]
    terms = jnp.stack([cos_f * cos_sum - sin_f * sin_sum, -(sin_f * cos_sum + cos_f * sin_sum)])
    return (surface_values, prior_spectra + terms)


def solution(mesh):
    return jax.shard_map(
        on_device,
        mesh=mesh,
        in_specs=(
            P(AXES, None, None),
            P(None, AXES),
            P(AXES),
            P(AXES, None),
            P(AXES),
            P(AXES),
            P(AXES),
            P(),
            P(),
            P(),
            P(),
            P(),
            P(None, None, AXES),
        ),
        out_specs=(P(None, AXES), P(None, None, AXES)),
        check_vma=False,
    )
```
